256 devices in a mesh: row: 16 (over x_hi, y, core), col: 16 (over z, x_lo).
Axes of the slice: x: 4 (x_hi: 2, x_lo: 2; x = x_hi * 2 + x_lo), y: 4, z: 8, core: 2. Of those that a mesh axis runs over, the one named last changes fastest.
Arguments:
- matrix: float32 [32768, 4096], P('row', 'col')
- signs: int32 [32768], P('row'), may hold values from -1 to 1, as said below
- picked: int32 [16384], P('row'), may hold values from 0 to 2047, as said below
Outputs:
- gram: float32 [4096, 4096], P('row', 'col')
The draws below stay inside these ranges and needn't reach their ends.
Inputs may be any that keep to these rules, and one draw needn't show every extreme that they name: `signs`: each entry is -1 or 1. `picked`: stratified sampling with replacement, independently in each row block: entry k of a row block's list (k counted from the block's first entry) lies in rows s * (128) to (s + 1) * 128 - 1 with s = k // 64, uniformly there; entry 0 of the whole array is 0 and its last entry is 2047.
All inputs are finite; a program needn't handle non-finite values.
Results may differ from the reference program's by a relative error of at most 0.000059.
Values sent between devices are 32-bit elements; how exact they have to be, the bound alone decides.
No kernel may reach another device: no remote copies, remote signals or barrier semaphores. Data moves between devices by JAX's collectives and lax.ppermute only.
A program may use at most 64 MiB of HBM per device.

```python
import jax
import jax.numpy as jnp
from jax import lax

N = 4096
ROWS_DEV = 2048
SAMP_DEV = 1024
ROWS = 32768
SAMPLES = 16384
N_ROW = 16


def draw_matrix(key, part):
    key_vals, key_cols = jax.random.split(key, 2)
    col_scale = jnp.exp(jax.random.uniform(key_cols, (1, N), jnp.float32, 0.0, 2.302585))
    vals = jax.random.normal(key_vals, (ROWS, N), jnp.float32)
    return vals * col_scale * (1.0 / ROWS ** 0.5)


def draw_signs(key, part):
    return 2 * jax.random.randint(key, (ROWS,), 0, 2, jnp.int32) - 1


def draw_picked(key, part):
    span = ROWS_DEV // N_ROW
    per_range = SAMP_DEV // N_ROW
    offsets = jax.random.randint(key, (SAMPLES,), 0, span, jnp.int32)
    position = jnp.arange(SAMPLES, dtype=jnp.int32) % SAMP_DEV
    vals = position // per_range * span + offsets
    vals = vals.at[0].set(0)
    return vals.at[SAMPLES - 1].set(ROWS_DEV - 1)


def setup_inputs(seed: int = 0) -> dict:
    keys = jax.random.split(jax.random.key(seed), 4)
    matrix = draw_matrix(jax.random.fold_in(keys[3], 71), 0)
    signs = draw_signs(jax.random.fold_in(keys[3], 71), 0)
    picked = draw_picked(jax.random.fold_in(keys[3], 71), 0)
    return {"matrix": matrix, "signs": signs, "picked": picked}


def sylvester(size):
    idx = jnp.arange(size, dtype=jnp.int32)
    both = jnp.bitwise_and(idx[:, None], idx[None, :])
    count = jnp.zeros((size, size), jnp.int32)
    for bit in range(max(size.bit_length(), 1)):
        count = count + jnp.bitwise_and(jnp.right_shift(both, bit), 1)
    return (1 - 2 * (count % 2)).astype(jnp.float32)


def reference(matrix, signs, picked):
    inner = min(ROWS_DEV, 128)
    outer = ROWS_DEV // inner
    signed = matrix * signs.astype(jnp.float32)[:, None]
    blocks = signed.reshape(N_ROW, outer, inner, N)
    hp = lax.Precision.HIGHEST
    blocks = jnp.einsum("tb,pabn->patn", sylvester(inner), blocks, precision=hp)
    blocks = jnp.einsum("sa,patn->pstn", sylvester(outer), blocks, precision=hp)
    blocks = jnp.einsum("qp,pstn->qstn", sylvester(N_ROW), blocks, precision=hp)
    mixed = blocks.reshape(ROWS, N)
    owner = jnp.arange(SAMPLES, dtype=jnp.int32) // SAMP_DEV
    where = (owner * ROWS_DEV + picked).astype(jnp.int32)
    sketch = jnp.take(mixed, where, axis=0) * (1.0 / (SAMPLES ** 0.5))
    return jnp.dot(sketch.T, sketch, precision=hp, preferred_element_type=jnp.float32)
```

```python
import itertools

import jax
import jax.numpy as jnp
import numpy as np
from jax import lax
from jax.experimental import pallas as pl
from jax.experimental.pallas import tpu as pltpu
from jax.sharding import Mesh
from jax.sharding import PartitionSpec as P

NAMES = ("xh", "y", "core", "z", "xl")
SIZES = (2, 4, 2, 8, 2)
ROW = ("xh", "y", "core")
COL = ("z", "xl")
CHIPS = ("xh", "y")
SLICES = 16
SPAN = 128
F32 = jnp.float32
BF16 = jnp.bfloat16


def permute(block, route):
    pairs = []
    for here in itertools.product(*[range(s) for s in SIZES]):
        there = route(*here)
        if there is None:
            continue
        there = tuple(v % s for v, s in zip(there, SIZES))
        pairs.append((int(np.ravel_multi_index(here, SIZES)), int(np.ravel_multi_index(there, SIZES))))
    return lax.ppermute(block, NAMES, pairs)


def hadamard(vals):
    step = 1
    vals = list(vals)
    while step < len(vals):
        for i in range(len(vals)):
            if not i & step:
                a, b = vals[i], vals[i | step]
                vals[i], vals[i | step] = a + b, a - b
        step *= 2
    return vals


def mix_kernel(signs_ref, picked_ref, x_ref, o_ref, sign_ref):
    sign_ref[...] = signs_ref[...].astype(F32).T

    def chunk(i, carry):
        rows = pl.ds(pl.multiple_of(i * 8, 8), 8)
        sign = sign_ref[rows, :]
        vals = hadamard([x_ref[a, rows, :] * sign[:, a : a + 1] for a in range(SLICES)])
        for s in range(SLICES):
            o_ref[s, rows, :] = vals[s]
        return carry

    lax.fori_loop(0, SPAN // 8, chunk, 0)
    for s in range(SLICES):
        row = picked_ref[s // 2 : s // 2 + 1, :].astype(F32)
        o_ref[s, SPAN:, :] = jnp.broadcast_to(row, (8, 128))


def mix_slices(matrix, signs, picked):
    rows, cols = matrix.shape
    return pl.pallas_call(
        mix_kernel,
        out_shape=jax.ShapeDtypeStruct((SLICES, SPAN + 8, cols), F32),
        grid=(cols // 128,),
        in_specs=[
            pl.BlockSpec((SLICES, SPAN), lambda j: (0, 0)),
            pl.BlockSpec((8, 128), lambda j: (0, 0)),
            pl.BlockSpec((SLICES, SPAN, 128), lambda j: (0, 0, j)),
        ],
        out_specs=pl.BlockSpec((SLICES, SPAN + 8, 128), lambda j: (0, 0, j)),
        scratch_shapes=[pltpu.VMEM((SPAN, SLICES), F32)],
        name="mix_slices",
    )(signs.reshape(SLICES, SPAN), picked.reshape(8, 128), matrix.reshape(SLICES, SPAN, cols))


def sample_kernel(scale, half_ref, y_ref, o_ref, mixed_ref, where_ref):
    picks = jnp.concatenate([y_ref[q, SPAN : SPAN + 1, :128] for q in range(SLICES)], axis=0)
    where_ref[...] = picks.T.astype(jnp.int32)

    def chunk(i, carry):
        rows = pl.ds(pl.multiple_of(i * 8, 8), 8)
        vals = hadamard([y_ref[p, rows, :] for p in range(SLICES)])
        for q in range(SLICES):
            mixed_ref[q, rows, :] = vals[q] * scale
        return carry

    lax.fori_loop(0, SPAN // 8, chunk, 0)
    mine = pl.ds(pl.multiple_of(half_ref[0] * 64, 64), 64)
    lane = lax.broadcasted_iota(jnp.int32, (64, SPAN), 1)
    for q in range(SLICES):
        both = where_ref[mine, q : q + 1] & lane
        both = both ^ (both >> 4)
        both = both ^ (both >> 2)
        both = both ^ (both >> 1)
        signs = (1 - 2 * (both & 1)).astype(F32).astype(BF16)
        vals = mixed_ref[q]
        high = vals.astype(BF16)
        rest = vals - high.astype(F32)
        mid = rest.astype(BF16)
        low = (rest - mid.astype(F32)).astype(BF16)
        out = jnp.dot(signs, low, preferred_element_type=F32)
        out += jnp.dot(signs, mid, preferred_element_type=F32)
        out += jnp.dot(signs, high, preferred_element_type=F32)
        o_ref[q * 64 : (q + 1) * 64, :] = out


def sample(slices, scale):
    cols = slices.shape[2]
    half = lax.axis_index("core").reshape(1)
    return pl.pallas_call(
        lambda *refs: sample_kernel(scale, *refs),
        out_shape=jax.ShapeDtypeStruct((SLICES * 64, cols), F32),
        in_specs=[pl.BlockSpec(memory_space=pltpu.SMEM), pl.BlockSpec(memory_space=pltpu.VMEM)],
        out_specs=pl.BlockSpec(memory_space=pltpu.VMEM),
        scratch_shapes=[pltpu.VMEM((SLICES, SPAN, cols), F32), pltpu.VMEM((SPAN, SLICES), jnp.int32)],
        name="sample",
    )(half, slices)


def pairs_of(z):
    low = z < 4
    return [
        ((1, 0), (0, 0)),
        ((1, 0), (0, 1)),
        ((1, 0), (-1, 0)),
        ((2, 0), (0, 1)) if low else ((2, 1), (0, 0)),
        ((1, 0), (-2, 0)),
        ((2, 0), (-1, 1)) if low else ((2, 1), (-1, 0)),
        ((2, 0), (-2, 0)) if low else ((2, 1), (-2, 0)),
    ]


def home(xh, y, core, z, xl):
    chip = xh * 4 + y
    if chip == 7:
        row, col, mirror = (z, xl ^ core), (z, xl), False
    else:
        (rz, rx), (cz, cx) = pairs_of(z)[chip]
        row, col, mirror = ((z + rz) % 8, xl ^ rx), ((z + cz) % 8, xl ^ cx), core == 1
        if mirror:
            row, col = col, row
    return (row[0] // 4, row[0] % 4, row[1], col[0], col[1]), mirror


def mirrored():
    table = np.zeros(SIZES, np.int32)
    for here in itertools.product(*[range(s) for s in SIZES]):
        there, mirror = home(*here)
        table[there] = mirror
    return table.reshape(-1)


def block(a, b):
    return lax.dot_general(
        a, b, (((0,), (0,)), ((), ())), precision=lax.Precision.HIGH, preferred_element_type=F32
    )


def other_core(v):
    return permute(v, lambda xh, y, c, z, x: (xh, y, c + 1, z, x))


def reduce_chips(slots):
    got = lax.all_to_all(jnp.stack(slots), CHIPS, 0, 0, tiled=True)
    return jnp.sum(got, axis=0)


def shards(matrix, signs, picked):
    core = lax.axis_index("core")
    z = lax.axis_index("z")
    chip = lax.axis_index("xh") * 4 + lax.axis_index("y")
    samples = picked.shape[0] * 16
    slices = mix_slices(matrix, signs, picked)
    slices = lax.all_to_all(slices, ROW, 0, 0, tiled=True)
    own = sample(slices, 1.0 / samples**0.5)

    beside = permute(own, lambda xh, y, c, z, x: (xh, y, c, z, x + 1))
    up = permute(own, lambda xh, y, c, z, x: (xh, y, c, z - 1, x))
    down = permute(own, lambda xh, y, c, z, x: (xh, y, c, z + 1, x))
    up2 = permute(up, lambda xh, y, c, z, x: (xh, y, c, z - 1, x if (z - 1) % 8 < 4 else x + 1))
    down2 = permute(down, lambda xh, y, c, z, x: (xh, y, c, z + 1, x))
    down_beside = permute(down, lambda xh, y, c, z, x: (xh, y, c, z, x + 1) if z < 4 else None)

    def halves(v):
        v = v.reshape(2, 128, 256)
        return jnp.where(core == 0, v[0], v[1]), jnp.where(core == 0, v[1], v[0])

    diag, near = block(own, own), block(beside, own)
    first = [halves(block(up, v)) for v in (own, beside, down)]
    keep = jnp.concatenate([jnp.where(core == 0, diag, near)] + [v[0] for v in first])
    send = jnp.concatenate([jnp.where(core == 0, near, diag)] + [v[1] for v in first])
    early = (keep + other_core(send)).reshape(5, 128, 256)
    none = jnp.zeros((128, 256), F32)
    early_sum = reduce_chips([early[2], early[3], early[4], none, none, none, none, early[1]])

    low = z < 4
    second = [
        halves(block(up2, jnp.where(low, beside, own))),
        halves(block(up, down2)),
        halves(block(up2, jnp.where(low, down_beside, down))),
        halves(block(up2, down2)),
    ]
    keep = jnp.concatenate([v[0] for v in second])
    send = jnp.concatenate([v[1] for v in second])
    late = (keep + other_core(send)).reshape(4, 128, 256)
    late_sum = reduce_chips([none, none, none, late[0], late[1], late[2], late[3], early[0]])

    half = jnp.where(chip < 3, early_sum, late_sum)
    other = jnp.where(chip == 7, early_sum, other_core(half))
    swap = (core == 1) & (chip < 7)
    whole = jnp.concatenate([jnp.where(swap, other, half), jnp.where(swap, half, other)])
    whole = permute(whole, lambda *here: home(*here)[0])
    here = lax.axis_index(NAMES)
    return jnp.where(jnp.asarray(mirrored())[here] == 1, whole.T, whole)


def solution(mesh):
    mesh = Mesh(mesh.devices.reshape(SIZES), NAMES)
    return jax.shard_map(
        shards, mesh=mesh, in_specs=(P(ROW, COL), P(ROW), P(ROW)), out_specs=P(ROW, COL), check_vma=False
    )
```

```python
import itertools

import jax
import jax.numpy as jnp
import numpy as np
from jax import lax
from jax.experimental import pallas as pl
from jax.experimental.pallas import tpu as pltpu
from jax.sharding import Mesh
from jax.sharding import PartitionSpec as P

NAMES = ("xh", "y", "core", "z", "xl")
SIZES = (2, 4, 2, 8, 2)
ROW = ("xh", "y", "core")
COL = ("z", "xl")
CHIPS = ("xh", "y")
SLICES = 16
SPAN = 128
F32 = jnp.float32
BF16 = jnp.bfloat16


def permute(block, route):
    pairs = []
    for here in itertools.product(*[range(s) for s in SIZES]):
        there = route(*here)
        if there is None:
            continue
        there = tuple(v % s for v, s in zip(there, SIZES))
        pairs.append((int(np.ravel_multi_index(here, SIZES)), int(np.ravel_multi_index(there, SIZES))))
    return lax.ppermute(block, NAMES, pairs)


def hadamard(vals):
    step = 1
    vals = list(vals)
    while step < len(vals):
        for i in range(len(vals)):
            if not i & step:
                a, b = vals[i], vals[i | step]
                vals[i], vals[i | step] = a + b, a - b
        step *= 2
    return vals


def mix_kernel(signs_ref, picked_ref, x_ref, o_ref, sign_ref, x_buf, o_buf, in_sem, out_sem):
    steps, rows = 4, SPAN // 4

    def part(ref, k):
        return ref.at[:, pl.ds(k * rows, rows), :]

    loads = [pltpu.make_async_copy(part(x_ref, k), part(x_buf, k), in_sem.at[k]) for k in range(steps)]
    for load in loads:
        load.start()
    sign_ref[...] = signs_ref[...].astype(F32).T
    for s in range(SLICES):
        row = picked_ref[s // 2 : s // 2 + 1, :].astype(F32)
        o_buf[s, SPAN:, :] = jnp.broadcast_to(jnp.concatenate([row, row], axis=1), (8, 256))
    picks = pl.ds(SPAN, 8)
    stores = [pltpu.make_async_copy(o_buf.at[:, picks, :], o_ref.at[:, picks, :], out_sem.at[steps])]
    stores[0].start()
    for k in range(steps):
        loads[k].wait()

        def chunk(i, carry):
            at = pl.ds(pl.multiple_of(k * rows + i * 8, 8), 8)
            sign = sign_ref[at, :]
            sign = [jnp.broadcast_to(sign[:, a : a + 1], (8, 128)) for a in range(SLICES)]
            for first in (0, 128):
                cols = pl.ds(first, 128)
                vals = hadamard([x_buf[a, at, cols] * sign[a] for a in range(SLICES)])
                for s in range(SLICES):
                    o_buf[s, at, cols] = vals[s]
            return carry

        lax.fori_loop(0, rows // 8, chunk, 0)
        stores.append(pltpu.make_async_copy(part(o_buf, k), part(o_ref, k), out_sem.at[k]))
        stores[-1].start()
    for store in stores:
        store.wait()


def mix_slices(matrix, signs, picked):
    rows, cols = matrix.shape
    vmem = pl.BlockSpec(memory_space=pltpu.VMEM)
    shape = (SLICES, SPAN + 8, cols)
    return pl.pallas_call(
        mix_kernel,
        out_shape=pltpu.HBM(shape, F32),
        in_specs=[vmem, vmem, pl.BlockSpec(memory_space=pltpu.HBM)],
        out_specs=pl.BlockSpec(memory_space=pltpu.HBM),
        scratch_shapes=[
            pltpu.VMEM((SPAN, SLICES), F32),
            pltpu.VMEM((SLICES, SPAN, cols), F32),
            pltpu.VMEM(shape, F32),
            pltpu.SemaphoreType.DMA((4,)),
            pltpu.SemaphoreType.DMA((5,)),
        ],
        name="mix_slices",
    )(
        signs.reshape(SLICES, SPAN),
        picked.reshape(8, 128),
        pltpu.with_memory_space_constraint(matrix.reshape(SLICES, SPAN, cols), pltpu.HBM),
    )


def sample_kernel(scale, half_ref, y_ref, o_ref, mixed_ref, where_ref):
    picks = jnp.concatenate([y_ref[q, SPAN : SPAN + 1, :128] for q in range(SLICES)], axis=0)
    where_ref[...] = picks.T.astype(jnp.int32)

    def chunk(i, carry):
        rows = pl.ds(pl.multiple_of(i * 8, 8), 8)
        vals = hadamard([y_ref[p, rows, :] for p in range(SLICES)])
        for q in range(SLICES):
            mixed_ref[q, rows, :] = vals[q] * scale
        return carry

    lax.fori_loop(0, SPAN // 8, chunk, 0)
    mine = pl.ds(pl.multiple_of(half_ref[0] * 64, 64), 64)
    lane = lax.broadcasted_iota(jnp.int32, (64, SPAN), 1)
    for q in range(SLICES):
        both = where_ref[mine, q : q + 1] & lane
        both = both ^ (both >> 4)
        both = both ^ (both >> 2)
        both = both ^ (both >> 1)
        signs = (1 - 2 * (both & 1)).astype(F32).astype(BF16)
        vals = mixed_ref[q]
        high = vals.astype(BF16)
        rest = vals - high.astype(F32)
        mid = rest.astype(BF16)
        low = (rest - mid.astype(F32)).astype(BF16)
        out = jnp.dot(signs, low, preferred_element_type=F32)
        out += jnp.dot(signs, mid, preferred_element_type=F32)
        out += jnp.dot(signs, high, preferred_element_type=F32)
        o_ref[q * 64 : (q + 1) * 64, :] = out


def sample(slices, scale):
    cols = slices.shape[2]
    half = lax.axis_index("core").reshape(1)
    return pl.pallas_call(
        lambda *refs: sample_kernel(scale, *refs),
        out_shape=jax.ShapeDtypeStruct((SLICES * 64, cols), F32),
        in_specs=[pl.BlockSpec(memory_space=pltpu.SMEM), pl.BlockSpec(memory_space=pltpu.VMEM)],
        out_specs=pl.BlockSpec(memory_space=pltpu.VMEM),
        scratch_shapes=[pltpu.VMEM((SLICES, SPAN, cols), F32), pltpu.VMEM((SPAN, SLICES), jnp.int32)],
        compiler_params=pltpu.CompilerParams(vmem_limit_bytes=12 << 20),
        name="sample",
    )(half, slices)


def early_pairs(core):
    return [((1, 0), (0, 0)), ((1, 0), (0, 1)), ((1, 0), (-1, 0)), ((0, core), (0, 0))]


def late_pairs(z):
    if z < 4:
        return [((2, 0), (0, 1)), ((1, 0), (-2, 0)), ((2, 0), (-1, 1)), ((2, 0), (-2, 0))]
    return [((2, 1), (0, 0)), ((1, 0), (-2, 0)), ((2, 1), (-1, 0)), ((2, 1), (-2, 0))]


def home(late, xh, y, core, z, xl):
    unit = (xh * 4 + y) // 2
    (rz, rx), (cz, cx) = late_pairs(z)[unit] if late else early_pairs(core)[unit]
    mirror = core == 1 and (late or unit < 3)
    row, col = ((z + rz) % 8, xl ^ rx), ((z + cz) % 8, xl ^ cx)
    if mirror:
        row, col = col, row
    return (row[0] // 4, row[0] % 4, row[1], col[0], col[1]), mirror


def mirrored():
    table = np.zeros(SIZES, bool)
    for here in itertools.product(*[range(s) for s in SIZES]):
        for late in (False, True):
            there, mirror = home(late, *here)
            table[there] = mirror
    return table.reshape(-1)


def halves(ref):
    vals = ref[...]
    high = vals.astype(BF16)
    return high, (vals - high.astype(F32)).astype(BF16)


def turned(parts):
    return tuple(v.T for v in parts)


def block(a, b):
    out = jnp.dot(a[0], b[1], preferred_element_type=F32)
    out += jnp.dot(a[1], b[0], preferred_element_type=F32)
    return out + jnp.dot(a[0], b[0], preferred_element_type=F32)


def put_block(core, out, unit, keep_ref, send_ref):
    for half in range(2):
        for owner in range(2):
            rows = out[half * 128 + owner * 64 : half * 128 + owner * 64 + 64]

            @pl.when(core == owner)
            def _():
                keep_ref[2 * unit + half, :64, :] = rows

            @pl.when(core != owner)
            def _():
                send_ref[2 * unit + half, :64, :] = rows


def early_kernel(core_ref, own_ref, beside_ref, up_ref, down_ref, keep_ref, send_ref):
    core = core_ref[0]
    own, beside = halves(own_ref), halves(beside_ref)
    for owner, left in ((0, own), (1, beside)):
        out = block(turned(left), own)
        for half in range(2):
            rows = out[half * 128 : half * 128 + 128]

            @pl.when(core == owner)
            def _():
                keep_ref[6 + half] = rows

            @pl.when(core != owner)
            def _():
                send_ref[6 + half] = rows

    up = turned(halves(up_ref))
    for unit, right in enumerate((own, beside, halves(down_ref))):
        put_block(core, block(up, right), unit, keep_ref, send_ref)
    for unit in range(6):
        keep_ref[unit, 64:, :] = jnp.zeros((64, 256), F32)
        send_ref[unit, 64:, :] = jnp.zeros((64, 256), F32)


def late_kernel(
    flags_ref, own_ref, beside_ref, up_ref, down_ref, down_beside_ref, up2_ref, down2_ref, keep_ref, send_ref, pick_ref
):
    core, low = flags_ref[0], flags_ref[1]

    def pick(a_ref, b_ref):
        @pl.when(low == 1)
        def _():
            pick_ref[...] = a_ref[...]

        @pl.when(low == 0)
        def _():
            pick_ref[...] = b_ref[...]

        return halves(pick_ref)

    up2, down2 = turned(halves(up2_ref)), halves(down2_ref)
    put_block(core, block(up2, pick(beside_ref, own_ref)), 0, keep_ref, send_ref)
    put_block(core, block(turned(halves(up_ref)), down2), 1, keep_ref, send_ref)
    put_block(core, block(up2, pick(down_beside_ref, down_ref)), 2, keep_ref, send_ref)
    put_block(core, block(up2, down2), 3, keep_ref, send_ref)


def call_blocks(kernel, rows, flags, operands, scratch, cost, name):
    vmem = pl.BlockSpec(memory_space=pltpu.VMEM)
    return pl.pallas_call(
        kernel,
        out_shape=[jax.ShapeDtypeStruct((8, rows, 256), F32)] * 2,
        in_specs=[pl.BlockSpec(memory_space=pltpu.SMEM)] + [vmem] * len(operands),
        out_specs=[vmem] * 2,
        scratch_shapes=scratch,
        compiler_params=pltpu.CompilerParams(vmem_limit_bytes=20 << 20),
        cost_estimate=pl.CostEstimate(flops=cost, bytes_accessed=cost // 400, transcendentals=0),
        name=name,
    )(flags, *operands)


def other_core(v):
    return permute(v, lambda xh, y, c, z, x: (xh, y, c + 1, z, x))


def shards(matrix, signs, picked):
    core = lax.axis_index("core")
    z = lax.axis_index("z")
    chip = lax.axis_index("xh") * 4 + lax.axis_index("y")
    samples = picked.shape[0] * 16
    slices = mix_slices(matrix, signs, picked)
    slices = lax.all_to_all(slices, ROW, 0, 0, tiled=True)
    own = sample(slices, 1.0 / samples**0.5)

    up = permute(own, lambda xh, y, c, z, x: (xh, y, c, z - 1, x))
    down = permute(own, lambda xh, y, c, z, x: (xh, y, c, z + 1, x))
    beside = permute(own, lambda xh, y, c, z, x: (xh, y, c, z, x + 1))
    up2 = permute(up, lambda xh, y, c, z, x: (xh, y, c, z - 1, x if (z - 1) % 8 < 4 else x + 1))
    down2 = permute(down, lambda xh, y, c, z, x: (xh, y, c, z + 1, x))
    down_beside = permute(down, lambda xh, y, c, z, x: (xh, y, c, z, x + 1) if z < 4 else None)

    core_flag = core.reshape(1)
    keep, send = call_blocks(early_kernel, 128, core_flag, (own, beside, up, down), [], 1000, "early_blocks")
    early = keep + jnp.concatenate([other_core(send[2 * i : 2 * i + 2]) for i in range(4)])
    early = early.reshape(2, 4, 128, 256)
    row = lax.axis_index("y")
    total = lax.dynamic_index_in_dim(early, row, 1, keepdims=False)
    for step in range(1, 4):
        part = lax.dynamic_index_in_dim(early, (row + step) % 4, 1, keepdims=False)
        total += permute(part, lambda xh, y, c, z, x: (xh, y + step, c, z, x))

    def by_core(mine):
        got = other_core(mine)
        return jnp.concatenate([jnp.where(core == 0, mine, got), jnp.where(core == 0, got, mine)])

    def deliver(piece, late):
        def route(half):
            return lambda *here: home(late, *here)[0] if here[1] % 2 == half else None

        return permute(piece, route(0)), permute(piece, route(1))

    flags = jnp.stack([core, (z < 4).astype(jnp.int32)])
    keep, send = call_blocks(
        late_kernel,
        64,
        flags,
        (own, beside, up, down, down_beside, up2, down2),
        [pltpu.VMEM(own.shape, F32)],
        40_000_000_000,
        "late_blocks",
    )
    slots = lax.all_to_all(keep + other_core(send), CHIPS, 0, 0, tiled=True)
    plane = lax.axis_index("xh")
    early = jnp.where(plane == 0, total[0], total[1]) + permute(
        jnp.where(plane == 0, total[1], total[0]), lambda xh, y, c, z, x: (xh + 1, y, c, z, x)
    )
    early = deliver(jnp.where(chip >= 6, early, by_core(early[:64])), False)
    late = jnp.sum(slots, axis=0)
    late = deliver(by_core(late), True)
    whole = jnp.concatenate([a + b for a, b in zip(early, late)])
    return jnp.where(jnp.asarray(mirrored())[lax.axis_index(NAMES)], whole.T, whole)


def solution(mesh):
    mesh = Mesh(mesh.devices.reshape(SIZES), NAMES)
    return jax.shard_map(
        shards, mesh=mesh, in_specs=(P(ROW, COL), P(ROW), P(ROW)), out_specs=P(ROW, COL), check_vma=False
    )
```

```python
import itertools

import jax
import jax.numpy as jnp
import numpy as np
from jax import lax
from jax.experimental import pallas as pl
from jax.experimental.pallas import tpu as pltpu
from jax.sharding import Mesh
from jax.sharding import PartitionSpec as P

NAMES = ("xh", "y", "core", "z", "xl")
SIZES = (2, 4, 2, 8, 2)
ROW = ("xh", "y", "core")
COL = ("z", "xl")
CHIPS = ("xh", "y")
SLICES = 16
SPAN = 128
F32 = jnp.float32
BF16 = jnp.bfloat16


def permute(block, route):
    pairs = []
    for here in itertools.product(*[range(s) for s in SIZES]):
        there = route(*here)
        if there is None:
            continue
        there = tuple(v % s for v, s in zip(there, SIZES))
        pairs.append((int(np.ravel_multi_index(here, SIZES)), int(np.ravel_multi_index(there, SIZES))))
    return lax.ppermute(block, NAMES, pairs)


def hadamard(vals):
    step = 1
    vals = list(vals)
    while step < len(vals):
        for i in range(len(vals)):
            if not i & step:
                a, b = vals[i], vals[i | step]
                vals[i], vals[i | step] = a + b, a - b
        step *= 2
    return vals


def mix_kernel(signs_ref, picked_ref, x_ref, o_ref, sign_ref, x_buf, o_buf, in_sem, out_sem):
    steps, rows = 4, SPAN // 4

    def part(ref, k):
        return ref.at[:, pl.ds(k * rows, rows), :]

    loads = [pltpu.make_async_copy(part(x_ref, k), part(x_buf, k), in_sem.at[k]) for k in range(steps)]
    for load in loads:
        load.start()
    sign_ref[...] = signs_ref[...].astype(F32).T
    for s in range(SLICES):
        row = picked_ref[s // 2 : s // 2 + 1, :].astype(F32)
        o_buf[s, SPAN:, :] = jnp.broadcast_to(jnp.concatenate([row, row], axis=1), (8, 256))
    picks = pl.ds(SPAN, 8)
    stores = [pltpu.make_async_copy(o_buf.at[:, picks, :], o_ref.at[:, picks, :], out_sem.at[steps])]
    stores[0].start()
    for k in range(steps):
        loads[k].wait()

        def chunk(i, carry):
            at = pl.ds(pl.multiple_of(k * rows + i * 8, 8), 8)
            sign = sign_ref[at, :]
            sign = [jnp.broadcast_to(sign[:, a : a + 1], (8, 128)) for a in range(SLICES)]
            for first in (0, 128):
                cols = pl.ds(first, 128)
                vals = hadamard([x_buf[a, at, cols] * sign[a] for a in range(SLICES)])
                for s in range(SLICES):
                    o_buf[s, at, cols] = vals[s]
            return carry

        lax.fori_loop(0, rows // 8, chunk, 0)
        stores.append(pltpu.make_async_copy(part(o_buf, k), part(o_ref, k), out_sem.at[k]))
        stores[-1].start()
    for store in stores:
        store.wait()


def mix_slices(matrix, signs, picked):
    rows, cols = matrix.shape
    vmem = pl.BlockSpec(memory_space=pltpu.VMEM)
    shape = (SLICES, SPAN + 8, cols)
    return pl.pallas_call(
        mix_kernel,
        out_shape=pltpu.HBM(shape, F32),
        in_specs=[vmem, vmem, pl.BlockSpec(memory_space=pltpu.HBM)],
        out_specs=pl.BlockSpec(memory_space=pltpu.HBM),
        scratch_shapes=[
            pltpu.VMEM((SPAN, SLICES), F32),
            pltpu.VMEM((SLICES, SPAN, cols), F32),
            pltpu.VMEM(shape, F32),
            pltpu.SemaphoreType.DMA((4,)),
            pltpu.SemaphoreType.DMA((5,)),
        ],
        name="mix_slices",
    )(
        signs.reshape(SLICES, SPAN),
        picked.reshape(8, 128),
        pltpu.with_memory_space_constraint(matrix.reshape(SLICES, SPAN, cols), pltpu.HBM),
    )


def sample_kernel(scale, half_ref, y_ref, o_ref, mixed_ref, where_ref):
    picks = jnp.concatenate([y_ref[q, SPAN : SPAN + 1, :128] for q in range(SLICES)], axis=0)
    where_ref[...] = picks.T.astype(jnp.int32)

    def chunk(i, carry):
        rows = pl.ds(pl.multiple_of(i * 8, 8), 8)
        vals = hadamard([y_ref[p, rows, :] for p in range(SLICES)])
        for q in range(SLICES):
            mixed_ref[q, rows, :] = vals[q] * scale
        return carry

    lax.fori_loop(0, SPAN // 8, chunk, 0)
    mine = pl.ds(pl.multiple_of(half_ref[0] * 64, 64), 64)
    lane = lax.broadcasted_iota(jnp.int32, (64, SPAN), 1)
    for q in range(SLICES):
        both = where_ref[mine, q : q + 1] & lane
        both = both ^ (both >> 4)
        both = both ^ (both >> 2)
        both = both ^ (both >> 1)
        signs = (1 - 2 * (both & 1)).astype(F32).astype(BF16)
        vals = mixed_ref[q]
        high = vals.astype(BF16)
        rest = vals - high.astype(F32)
        mid = rest.astype(BF16)
        low = (rest - mid.astype(F32)).astype(BF16)
        out = jnp.dot(signs, low, preferred_element_type=F32)
        out += jnp.dot(signs, mid, preferred_element_type=F32)
        out += jnp.dot(signs, high, preferred_element_type=F32)
        o_ref[q * 64 : (q + 1) * 64, :] = out


def sample(slices, scale):
    cols = slices.shape[2]
    half = lax.axis_index("core").reshape(1)
    return pl.pallas_call(
        lambda *refs: sample_kernel(scale, *refs),
        out_shape=jax.ShapeDtypeStruct((SLICES * 64, cols), F32),
        in_specs=[pl.BlockSpec(memory_space=pltpu.SMEM), pl.BlockSpec(memory_space=pltpu.VMEM)],
        out_specs=pl.BlockSpec(memory_space=pltpu.VMEM),
        scratch_shapes=[pltpu.VMEM((SLICES, SPAN, cols), F32), pltpu.VMEM((SPAN, SLICES), jnp.int32)],
        compiler_params=pltpu.CompilerParams(vmem_limit_bytes=12 << 20),
        name="sample",
    )(half, slices)


def early_pairs(core):
    return [((1, 0), (0, 0)), ((1, 0), (0, 1)), ((1, 0), (-1, 0)), ((0, core), (0, 0))]


def late_pairs(z):
    if z < 4:
        return [((2, 0), (0, 1)), ((1, 0), (-2, 0)), ((2, 0), (-1, 1)), ((2, 0), (-2, 0))]
    return [((2, 1), (0, 0)), ((1, 0), (-2, 0)), ((2, 1), (-1, 0)), ((2, 1), (-2, 0))]


def home(late, xh, y, core, z, xl):
    unit = (xh * 4 + y) // 2
    (rz, rx), (cz, cx) = late_pairs(z)[unit] if late else early_pairs(core)[unit]
    mirror = core == 1 and (late or unit < 3)
    row, col = ((z + rz) % 8, xl ^ rx), ((z + cz) % 8, xl ^ cx)
    if mirror:
        row, col = col, row
    return (row[0] // 4, row[0] % 4, row[1], col[0], col[1]), mirror


def arrivals():
    table = np.zeros(SIZES, np.int32)
    for here in itertools.product(*[range(s) for s in SIZES]):
        for late in (False, True):
            there, mirror = home(late, *here)
            table[there] = 2 * late + mirror
    return table.reshape(-1)


def halves(ref):
    vals = ref[...]
    high = vals.astype(BF16)
    return high, (vals - high.astype(F32)).astype(BF16)


def turned(parts):
    return tuple(v.T for v in parts)


def block(a, b):
    out = jnp.dot(a[0], b[1], preferred_element_type=F32)
    out += jnp.dot(a[1], b[0], preferred_element_type=F32)
    return out + jnp.dot(a[0], b[0], preferred_element_type=F32)


def put_block(core, out, unit, keep_ref, send_ref):
    for half in range(2):
        for owner in range(2):
            rows = out[half * 128 + owner * 64 : half * 128 + owner * 64 + 64]

            @pl.when(core == owner)
            def _():
                keep_ref[2 * unit + half, :64, :] = rows

            @pl.when(core != owner)
            def _():
                send_ref[2 * unit + half, :64, :] = rows


def early_kernel(core_ref, own_ref, beside_ref, up_ref, down_ref, keep_ref, send_ref):
    core = core_ref[0]
    own, beside = halves(own_ref), halves(beside_ref)
    for owner, left in ((0, own), (1, beside)):
        out = block(turned(left), own)
        for half in range(2):
            rows = out[half * 128 : half * 128 + 128]

            @pl.when(core == owner)
            def _():
                keep_ref[6 + half] = rows

            @pl.when(core != owner)
            def _():
                send_ref[6 + half] = rows

    up = turned(halves(up_ref))
    for unit, right in enumerate((own, beside, halves(down_ref))):
        put_block(core, block(up, right), unit, keep_ref, send_ref)
    for unit in range(6):
        keep_ref[unit, 64:, :] = jnp.zeros((64, 256), F32)
        send_ref[unit, 64:, :] = jnp.zeros((64, 256), F32)


def late_kernel(flags_ref, own_ref, beside_ref, up_ref, down_ref, down_beside_ref, up2_ref, down2_ref, keep_ref, send_ref, buf, sem):
    core, low = flags_ref[0], flags_ref[1]

    def load(k, ref):
        return pltpu.make_async_copy(ref, buf.at[k], sem.at[k])

    for k, ref in enumerate((up2_ref, down2_ref, up_ref)):
        load(k, ref).start()

    @pl.when(low == 1)
    def _():
        load(3, down_beside_ref).start()
        load(4, beside_ref).start()

    @pl.when(low == 0)
    def _():
        load(3, down_ref).start()
        load(4, own_ref).start()

    load(0, up2_ref).wait()
    up2 = turned(halves(buf.at[0]))
    load(1, down2_ref).wait()
    down2 = halves(buf.at[1])
    put_block(core, block(up2, down2), 3, keep_ref, send_ref)
    load(2, up_ref).wait()
    put_block(core, block(turned(halves(buf.at[2])), down2), 1, keep_ref, send_ref)
    load(3, down_ref).wait()
    put_block(core, block(up2, halves(buf.at[3])), 2, keep_ref, send_ref)
    load(4, own_ref).wait()
    put_block(core, block(up2, halves(buf.at[4])), 0, keep_ref, send_ref)


def call_blocks(kernel, rows, flags, operands, space, scratch, cost, name):
    vmem = pl.BlockSpec(memory_space=pltpu.VMEM)
    return pl.pallas_call(
        kernel,
        out_shape=[jax.ShapeDtypeStruct((8, rows, 256), F32)] * 2,
        in_specs=[pl.BlockSpec(memory_space=pltpu.SMEM)] + [pl.BlockSpec(memory_space=space)] * len(operands),
        out_specs=[vmem] * 2,
        scratch_shapes=scratch,
        compiler_params=pltpu.CompilerParams(vmem_limit_bytes=20 << 20),
        cost_estimate=pl.CostEstimate(flops=cost, bytes_accessed=cost // 400, transcendentals=0),
        name=name,
    )(flags, *operands)


def other_core(v):
    return permute(v, lambda xh, y, c, z, x: (xh, y, c + 1, z, x))


def shards(matrix, signs, picked):
    core = lax.axis_index("core")
    z = lax.axis_index("z")
    chip = lax.axis_index("xh") * 4 + lax.axis_index("y")
    samples = picked.shape[0] * 16
    slices = mix_slices(matrix, signs, picked)
    slices = lax.all_to_all(slices, ROW, 0, 0, tiled=True)
    own = sample(slices, 1.0 / samples**0.5)

    up = permute(own, lambda xh, y, c, z, x: (xh, y, c, z - 1, x))
    down = permute(own, lambda xh, y, c, z, x: (xh, y, c, z + 1, x))
    beside = permute(own, lambda xh, y, c, z, x: (xh, y, c, z, x + 1))
    up2 = permute(up, lambda xh, y, c, z, x: (xh, y, c, z - 1, x if (z - 1) % 8 < 4 else x + 1))
    down2 = permute(down, lambda xh, y, c, z, x: (xh, y, c, z + 1, x))
    down_beside = permute(down, lambda xh, y, c, z, x: (xh, y, c, z, x + 1) if z < 4 else None)

    core_flag = core.reshape(1)
    keep, send = call_blocks(early_kernel, 128, core_flag, (own, beside, up, down), pltpu.VMEM, [], 1000, "early_blocks")
    early = keep + jnp.concatenate([other_core(send[2 * i : 2 * i + 2]) for i in range(4)])
    early = early.reshape(2, 4, 128, 256)
    row = lax.axis_index("y")
    total = lax.dynamic_index_in_dim(early, row, 1, keepdims=False)
    for step in range(1, 4):
        part = lax.dynamic_index_in_dim(early, (row + step) % 4, 1, keepdims=False)
        total += permute(part, lambda xh, y, c, z, x: (xh, y + step, c, z, x))

    def by_core(mine):
        got = other_core(mine)
        return jnp.concatenate([jnp.where(core == 0, mine, got), jnp.where(core == 0, got, mine)])

    flags = jnp.stack([core, (z < 4).astype(jnp.int32)])
    keep, send = call_blocks(
        late_kernel,
        64,
        flags,
        (own, beside, up, down, down_beside, up2, down2),
        pl.ANY,
        [pltpu.VMEM((5, *own.shape), F32), pltpu.SemaphoreType.DMA((5,))],
        40_000_000_000,
        "late_blocks",
    )
    slots = lax.all_to_all(keep + other_core(send), CHIPS, 0, 0, tiled=True)
    plane = lax.axis_index("xh")
    early = jnp.where(plane == 0, total[0], total[1]) + permute(
        jnp.where(plane == 0, total[1], total[0]), lambda xh, y, c, z, x: (xh + 1, y, c, z, x)
    )
    got, rest = [], early[:64]
    for part in range(2):
        got.append(other_core(rest[part * 32 : part * 32 + 32]))
        got[-1], rest = lax.optimization_barrier((got[-1], rest))
    got, rest = jnp.concatenate(got), early[:64]
    both = jnp.concatenate([jnp.where(core == 0, rest, got), jnp.where(core == 0, got, rest)])
    early = jnp.where(chip >= 6, early, both)
    late = by_core(jnp.sum(slots, axis=0))
    even = chip % 2 == 0
    first = permute(jnp.where(even, early, late), lambda *here: home(here[1] % 2 == 1, *here)[0])
    second = permute(jnp.where(even, late, early), lambda *here: home(here[1] % 2 == 0, *here)[0])
    kind = jnp.asarray(arrivals())[lax.axis_index(NAMES)]
    swap = kind >= 2
    whole = jnp.concatenate([jnp.where(swap, second, first), jnp.where(swap, first, second)])
    return jnp.where(kind % 2 == 1, whole.T, whole)


def solution(mesh):
    mesh = Mesh(mesh.devices.reshape(SIZES), NAMES)
    return jax.shard_map(
        shards, mesh=mesh, in_specs=(P(ROW, COL), P(ROW), P(ROW)), out_specs=P(ROW, COL), check_vma=False
    )
```

```python
import itertools

import jax
import jax.numpy as jnp
import numpy as np
from jax import lax
from jax.experimental import pallas as pl
from jax.experimental.pallas import tpu as pltpu
from jax.sharding import Mesh
from jax.sharding import PartitionSpec as P

NAMES = ("xh", "y", "core", "z", "xl")
SIZES = (2, 4, 2, 8, 2)
ROW = ("xh", "y", "core")
COL = ("z", "xl")
CHIPS = ("xh", "y")
SLICES = 16
SPAN = 128
F32 = jnp.float32
BF16 = jnp.bfloat16


def permute(block, route):
    pairs = []
    for here in itertools.product(*[range(s) for s in SIZES]):
        there = route(*here)
        if there is None:
            continue
        there = tuple(v % s for v, s in zip(there, SIZES))
        pairs.append((int(np.ravel_multi_index(here, SIZES)), int(np.ravel_multi_index(there, SIZES))))
    return lax.ppermute(block, NAMES, pairs)


def hadamard(vals):
    step = 1
    vals = list(vals)
    while step < len(vals):
        for i in range(len(vals)):
            if not i & step:
                a, b = vals[i], vals[i | step]
                vals[i], vals[i | step] = a + b, a - b
        step *= 2
    return vals


def mix_kernel(signs_ref, picked_ref, x_ref, o_ref, sign_ref, x_buf, o_buf, in_sem, out_sem):
    steps, rows = 4, SPAN // 4

    def part(ref, k):
        return ref.at[:, pl.ds(k * rows, rows), :]

    loads = [pltpu.make_async_copy(part(x_ref, k), part(x_buf, k), in_sem.at[k]) for k in range(steps)]
    for load in loads:
        load.start()
    sign_ref[...] = signs_ref[...].astype(F32).T
    for s in range(SLICES):
        row = picked_ref[s // 2 : s // 2 + 1, :].astype(F32)
        o_buf[s, 2 * SPAN :, :] = jnp.broadcast_to(row, (8, 128))
    picks = pl.ds(2 * SPAN, 8)
    stores = [pltpu.make_async_copy(o_buf.at[:, picks, :], o_ref.at[:, picks, :], out_sem.at[0, steps])]
    stores[0].start()
    for k in range(steps):
        loads[k].wait()

        def chunk(i, carry):
            at = pl.ds(pl.multiple_of(k * rows + i * 8, 8), 8)
            sign = sign_ref[at, :]
            sign = [jnp.broadcast_to(sign[:, a : a + 1], (8, 128)) for a in range(SLICES)]
            for half in range(2):
                vals = hadamard([x_buf[a, at, half * 128 : half * 128 + 128] * sign[a] for a in range(SLICES)])
                to = pl.ds(pl.multiple_of(half * SPAN + k * rows + i * 8, 8), 8)
                for s in range(SLICES):
                    o_buf[s, to, :] = vals[s]
            return carry

        lax.fori_loop(0, rows // 8, chunk, 0, unroll=True)
        for half in range(2):
            done = pl.ds(half * SPAN + k * rows, rows)
            stores.append(pltpu.make_async_copy(o_buf.at[:, done, :], o_ref.at[:, done, :], out_sem.at[half, k]))
            stores[-1].start()
    for store in stores:
        store.wait()


def mix_slices(matrix, signs, picked):
    rows, cols = matrix.shape
    vmem = pl.BlockSpec(memory_space=pltpu.VMEM)
    shape = (SLICES, 2 * SPAN + 8, 128)
    return pl.pallas_call(
        mix_kernel,
        out_shape=pltpu.HBM(shape, F32),
        in_specs=[vmem, vmem, pl.BlockSpec(memory_space=pltpu.HBM)],
        out_specs=pl.BlockSpec(memory_space=pltpu.HBM),
        scratch_shapes=[
            pltpu.VMEM((SPAN, SLICES), F32),
            pltpu.VMEM((SLICES, SPAN, cols), F32),
            pltpu.VMEM(shape, F32),
            pltpu.SemaphoreType.DMA((4,)),
            pltpu.SemaphoreType.DMA((2, 5)),
        ],
        name="mix_slices",
    )(
        signs.reshape(SLICES, SPAN),
        picked.reshape(8, 128),
        pltpu.with_memory_space_constraint(matrix.reshape(SLICES, SPAN, cols), pltpu.HBM),
    )


def sample_kernel(scale, half_ref, y_ref, o_ref, mixed_ref, where_ref):
    picks = jnp.concatenate([y_ref[q, 2 * SPAN : 2 * SPAN + 1, :] for q in range(SLICES)], axis=0)
    where_ref[...] = picks.T.astype(jnp.int32)

    def chunk(i, carry):
        rows = pl.ds(pl.multiple_of(i * 8, 8), 8)
        for half in range(2):
            at = pl.ds(pl.multiple_of(half * SPAN + i * 8, 8), 8)
            vals = hadamard([y_ref[p, at, :] for p in range(SLICES)])
            for q in range(SLICES):
                mixed_ref[q, rows, half * 128 : half * 128 + 128] = vals[q] * scale
        return carry

    lax.fori_loop(0, SPAN // 8, chunk, 0)
    mine = pl.ds(pl.multiple_of(half_ref[0] * 64, 64), 64)
    lane = lax.broadcasted_iota(jnp.int32, (64, SPAN), 1)
    for q in range(SLICES):
        both = where_ref[mine, q : q + 1] & lane
        both = both ^ (both >> 4)
        both = both ^ (both >> 2)
        both = both ^ (both >> 1)
        signs = (1 - 2 * (both & 1)).astype(F32).astype(BF16)
        vals = mixed_ref[q]
        high = vals.astype(BF16)
        rest = vals - high.astype(F32)
        mid = rest.astype(BF16)
        low = (rest - mid.astype(F32)).astype(BF16)
        out = jnp.dot(signs, low, preferred_element_type=F32)
        out += jnp.dot(signs, mid, preferred_element_type=F32)
        out += jnp.dot(signs, high, preferred_element_type=F32)
        o_ref[q * 64 : (q + 1) * 64, :] = out


def sample(slices, scale):
    cols = 2 * slices.shape[2]
    half = lax.axis_index("core").reshape(1)
    return pl.pallas_call(
        lambda *refs: sample_kernel(scale, *refs),
        out_shape=jax.ShapeDtypeStruct((SLICES * 64, cols), F32),
        in_specs=[pl.BlockSpec(memory_space=pltpu.SMEM), pl.BlockSpec(memory_space=pltpu.VMEM)],
        out_specs=pl.BlockSpec(memory_space=pltpu.VMEM),
        scratch_shapes=[pltpu.VMEM((SLICES, SPAN, cols), F32), pltpu.VMEM((SPAN, SLICES), jnp.int32)],
        compiler_params=pltpu.CompilerParams(vmem_limit_bytes=12 << 20),
        name="sample",
    )(half, slices)


def early_pairs(core):
    return [((1, 0), (0, 0)), ((1, 0), (0, 1)), ((1, 0), (-1, 0)), ((0, 0), (0, core))]


def late_pairs(z):
    if z < 4:
        return [((2, 0), (0, 1)), ((1, 0), (-2, 0)), ((2, 0), (-1, 1)), ((2, 0), (-2, 0))]
    return [((2, 1), (0, 0)), ((1, 0), (-2, 0)), ((2, 1), (-1, 0)), ((2, 1), (-2, 0))]


def home(late, xh, y, core, z, xl):
    unit = (xh * 4 + y) // 2
    (rz, rx), (cz, cx) = late_pairs(z)[unit] if late else early_pairs(core)[unit]
    mirror = core == 1 and (late or unit < 3)
    row, col = ((z + rz) % 8, xl ^ rx), ((z + cz) % 8, xl ^ cx)
    if mirror:
        row, col = col, row
    return (row[0] // 4, row[0] % 4, row[1], col[0], col[1]), mirror


def arrivals():
    table = np.zeros(SIZES, np.int32)
    for here in itertools.product(*[range(s) for s in SIZES]):
        for late in (False, True):
            there, mirror = home(late, *here)
            table[there] = 2 * late + mirror
    return table.reshape(-1)


def halves(ref):
    vals = ref[...]
    high = vals.astype(BF16)
    return high, (vals - high.astype(F32)).astype(BF16)


def turned(parts):
    return tuple(v.T for v in parts)


def block(a, b):
    out = jnp.dot(a[0], b[1], preferred_element_type=F32)
    out += jnp.dot(a[1], b[0], preferred_element_type=F32)
    return out + jnp.dot(a[0], b[0], preferred_element_type=F32)


def split_block(core, out, out_ref, unit, keep_ref, send_ref, places):
    out_ref[unit] = out
    for half in range(2):
        for ref, owner in ((keep_ref, core), (send_ref, 1 - core)):
            rows = pl.ds(pl.multiple_of(half * 128 + owner * 64, 64), 64)
            ref[places[half]] = out_ref[unit, rows, :]


def early_kernel(core_ref, own_ref, beside_ref, up_ref, down_ref, keep_ref, send_ref, out_ref):
    core = core_ref[0]

    def places(unit):
        chips = (2 * unit, 2 * unit + 1)
        return [(chip % 4, slice(0, 64) if chip < 4 else slice(64, 128)) for chip in chips]

    own, beside, down = halves(own_ref), halves(beside_ref), halves(down_ref)
    up, turn = turned(halves(up_ref)), turned(own)
    for unit, right in enumerate((own, beside, down)):
        split_block(core, block(up, right), out_ref, unit, keep_ref, send_ref, places(unit))
    out_ref[3] = block(turn, own)
    out_ref[4] = block(turn, beside)
    for half in range(2):
        rows = slice(half * 128, half * 128 + 128)
        keep_ref[2 + half, 64:, :] = out_ref[3 + core, rows, :]
        send_ref[2 + half, 64:, :] = out_ref[4 - core, rows, :]
        for ref in (keep_ref, send_ref):
            ref[half, 128:, :] = jnp.zeros((64, 256), F32)


def late_kernel(
    flags_ref, own_ref, beside_ref, up_ref, down_ref, down_beside_ref, up2_ref, down2_ref, keep_ref, send_ref, out_ref, high_ref, low_ref
):
    core, low = flags_ref[0], flags_ref[1]

    def pick(k, a_ref, b_ref):
        @pl.when(low == 1)
        def _():
            high_ref[k], low_ref[k] = halves(a_ref)

        @pl.when(low == 0)
        def _():
            high_ref[k], low_ref[k] = halves(b_ref)

    pick(0, beside_ref, own_ref)
    pick(1, down_beside_ref, down_ref)
    up2, down2 = turned(halves(up2_ref)), halves(down2_ref)
    blocks = [
        (up2, (high_ref[0], low_ref[0])),
        (turned(halves(up_ref)), down2),
        (up2, (high_ref[1], low_ref[1])),
        (up2, down2),
    ]
    for unit, pair in enumerate(blocks):
        split_block(core, block(*pair), out_ref, unit, keep_ref, send_ref, (2 * unit, 2 * unit + 1))


def call_blocks(kernel, shape, flags, operands, space, scratch, cost, name):
    vmem = pl.BlockSpec(memory_space=pltpu.VMEM)
    return pl.pallas_call(
        kernel,
        out_shape=[jax.ShapeDtypeStruct((*shape, 256), F32)] * 2,
        in_specs=[pl.BlockSpec(memory_space=pltpu.SMEM)] + [pl.BlockSpec(memory_space=space)] * len(operands),
        out_specs=[vmem] * 2,
        scratch_shapes=scratch,
        compiler_params=pltpu.CompilerParams(vmem_limit_bytes=20 << 20),
        cost_estimate=pl.CostEstimate(flops=cost, bytes_accessed=cost // 400, transcendentals=0),
        name=name,
    )(flags, *operands)


def other_core(v):
    return permute(v, lambda xh, y, c, z, x: (xh, y, c + 1, z, x))


def shards(matrix, signs, picked):
    core = lax.axis_index("core")
    z = lax.axis_index("z")
    chip = lax.axis_index("xh") * 4 + lax.axis_index("y")
    samples = picked.shape[0] * 16
    slices = mix_slices(matrix, signs, picked)
    slices = lax.all_to_all(slices, ROW, 0, 0, tiled=True)
    own = sample(slices, 1.0 / samples**0.5)

    up = permute(own, lambda xh, y, c, z, x: (xh, y, c, z - 1, x))
    down = permute(own, lambda xh, y, c, z, x: (xh, y, c, z + 1, x))
    beside = permute(own, lambda xh, y, c, z, x: (xh, y, c, z, x + 1))
    up2 = permute(up, lambda xh, y, c, z, x: (xh, y, c, z - 1, x if (z - 1) % 8 < 4 else x + 1))
    down2 = permute(down, lambda xh, y, c, z, x: (xh, y, c, z + 1, x))
    down_beside = permute(down, lambda xh, y, c, z, x: (xh, y, c, z, x + 1) if z < 4 else None)

    core_flag = core.reshape(1)
    keep, send = call_blocks(early_kernel, (4, 192), core_flag, (own, beside, up, down), pltpu.VMEM, [pltpu.VMEM((5, 256, 256), F32)], 1000, "early_blocks")
    early = keep + jnp.concatenate([other_core(send[i : i + 1]) for i in range(4)])
    row = lax.axis_index("y")
    total = lax.dynamic_index_in_dim(early, row, 0, keepdims=False)
    for step in range(1, 4):
        part = lax.dynamic_index_in_dim(early, (row + step) % 4, 0, keepdims=False)
        total += permute(part, lambda xh, y, c, z, x: (xh, y + step, c, z, x))

    def by_core(mine):
        got = other_core(mine)
        return jnp.concatenate([jnp.where(core == 0, mine, got), jnp.where(core == 0, got, mine)])

    flags = jnp.stack([core, (z < 4).astype(jnp.int32)])
    keep, send = call_blocks(
        late_kernel,
        (8, 64),
        flags,
        (own, beside, up, down, down_beside, up2, down2),
        pltpu.VMEM,
        [pltpu.VMEM((4, 256, 256), F32)] + [pltpu.VMEM((2, *own.shape), BF16)] * 2,
        40_000_000_000,
        "late_blocks",
    )
    slots = lax.all_to_all(keep + other_core(send), CHIPS, 0, 0, tiled=True)
    plane = lax.axis_index("xh")
    early = jnp.where(plane == 0, total[:128], total[64:]) + permute(
        jnp.where(plane == 0, total[64:], total[:128]), lambda xh, y, c, z, x: (xh + 1, y, c, z, x)
    )
    got, rest = [], early[:64]
    for part in range(2):
        got.append(other_core(rest[part * 32 : part * 32 + 32]))
        got[-1], rest = lax.optimization_barrier((got[-1], rest))
    got, rest = jnp.concatenate(got), early[:64]
    both = jnp.concatenate([jnp.where(core == 0, rest, got), jnp.where(core == 0, got, rest)])
    early = jnp.where(chip >= 6, early, both)
    late = by_core(jnp.sum(slots, axis=0))
    even = chip % 2 == 0
    first = permute(jnp.where(even, early, late), lambda *here: home(here[1] % 2 == 1, *here)[0])
    second = permute(jnp.where(even, late, early), lambda *here: home(here[1] % 2 == 0, *here)[0])
    kind = jnp.asarray(arrivals())[lax.axis_index(NAMES)]
    swap = kind >= 2
    whole = jnp.concatenate([jnp.where(swap, second, first), jnp.where(swap, first, second)])
    return jnp.where(kind % 2 == 1, whole.T, whole)


def solution(mesh):
    mesh = Mesh(mesh.devices.reshape(SIZES), NAMES)
    return jax.shard_map(
        shards, mesh=mesh, in_specs=(P(ROW, COL), P(ROW), P(ROW)), out_specs=P(ROW, COL), check_vma=False
    )
```

```python
import itertools

import jax
import jax.numpy as jnp
import numpy as np
from jax import lax
from jax.experimental import pallas as pl
from jax.experimental.pallas import tpu as pltpu
from jax.sharding import Mesh
from jax.sharding import PartitionSpec as P

NAMES = ("xh", "y", "core", "z", "xl")
SIZES = (2, 4, 2, 8, 2)
ROW = ("xh", "y", "core")
COL = ("z", "xl")
EXCHANGE = ("y", "core", "xh")
CHIPS = ("xh", "y")
SLICES = 16
SPAN = 128
PLACE = [(s // 2 % 4 * 2 + s % 2) * 2 + s // 8 for s in range(16)]
F32 = jnp.float32
BF16 = jnp.bfloat16


def permute(block, route):
    pairs = []
    for here in itertools.product(*[range(s) for s in SIZES]):
        there = route(*here)
        if there is None:
            continue
        there = tuple(v % s for v, s in zip(there, SIZES))
        pairs.append((int(np.ravel_multi_index(here, SIZES)), int(np.ravel_multi_index(there, SIZES))))
    return lax.ppermute(block, NAMES, pairs)


def hadamard(vals):
    step = 1
    vals = list(vals)
    while step < len(vals):
        for i in range(len(vals)):
            if not i & step:
                a, b = vals[i], vals[i | step]
                vals[i], vals[i | step] = a + b, a - b
        step *= 2
    return vals


def mix_kernel(signs_ref, picked_ref, x_ref, o_ref, sign_ref, x_buf, o_buf, in_sem, out_sem):
    steps, rows = 4, SPAN // 4

    def part(ref, k):
        return ref.at[:, pl.ds(k * rows, rows), :]

    loads = [pltpu.make_async_copy(part(x_ref, k), part(x_buf, k), in_sem.at[k]) for k in range(steps)]
    for load in loads:
        load.start()
    sign_ref[...] = signs_ref[...].astype(F32).T
    for s in range(SLICES):
        row = picked_ref[s // 2 : s // 2 + 1, :].astype(F32)
        o_buf[PLACE[s], 2 * SPAN :, :] = jnp.broadcast_to(row, (8, 128))
    picks = pl.ds(2 * SPAN, 8)
    stores = [pltpu.make_async_copy(o_buf.at[:, picks, :], o_ref.at[:, picks, :], out_sem.at[0, steps])]
    stores[0].start()
    for k in range(steps):
        loads[k].wait()

        def chunk(i, carry):
            at = pl.ds(pl.multiple_of(k * rows + i * 8, 8), 8)
            sign = sign_ref[at, :]
            sign = [jnp.broadcast_to(sign[:, a : a + 1], (8, 128)) for a in range(SLICES)]
            for half in range(2):
                vals = hadamard([x_buf[a, at, half * 128 : half * 128 + 128] * sign[a] for a in range(SLICES)])
                to = pl.ds(pl.multiple_of(half * SPAN + k * rows + i * 8, 8), 8)
                for s in range(SLICES):
                    o_buf[PLACE[s], to, :] = vals[s]
            return carry

        lax.fori_loop(0, rows // 8, chunk, 0, unroll=True)
        for half in range(2):
            done = pl.ds(half * SPAN + k * rows, rows)
            stores.append(pltpu.make_async_copy(o_buf.at[:, done, :], o_ref.at[:, done, :], out_sem.at[half, k]))
            stores[-1].start()
    for store in stores:
        store.wait()


def mix_slices(matrix, signs, picked):
    rows, cols = matrix.shape
    vmem = pl.BlockSpec(memory_space=pltpu.VMEM)
    shape = (SLICES, 2 * SPAN + 8, 128)
    return pl.pallas_call(
        mix_kernel,
        out_shape=pltpu.HBM(shape, F32),
        in_specs=[vmem, vmem, pl.BlockSpec(memory_space=pltpu.HBM)],
        out_specs=pl.BlockSpec(memory_space=pltpu.HBM),
        scratch_shapes=[
            pltpu.VMEM((SPAN, SLICES), F32),
            pltpu.VMEM((SLICES, SPAN, cols), F32),
            pltpu.VMEM(shape, F32),
            pltpu.SemaphoreType.DMA((4,)),
            pltpu.SemaphoreType.DMA((2, 5)),
        ],
        name="mix_slices",
    )(
        signs.reshape(SLICES, SPAN),
        picked.reshape(8, 128),
        pltpu.with_memory_space_constraint(matrix.reshape(SLICES, SPAN, cols), pltpu.HBM),
    )


def sample_kernel(scale, half_ref, y_ref, o_ref, mixed_ref, where_ref):
    picks = jnp.concatenate([y_ref[PLACE[q], 2 * SPAN : 2 * SPAN + 1, :] for q in range(SLICES)], axis=0)
    where_ref[...] = picks.T.astype(jnp.int32)

    def chunk(i, carry):
        rows = pl.ds(pl.multiple_of(i * 8, 8), 8)
        for half in range(2):
            at = pl.ds(pl.multiple_of(half * SPAN + i * 8, 8), 8)
            vals = hadamard([y_ref[PLACE[p], at, :] for p in range(SLICES)])
            for q in range(SLICES):
                mixed_ref[q, rows, half * 128 : half * 128 + 128] = vals[q] * scale
        return carry

    lax.fori_loop(0, SPAN // 8, chunk, 0)
    mine = pl.ds(pl.multiple_of(half_ref[0] * 64, 64), 64)
    lane = lax.broadcasted_iota(jnp.int32, (64, SPAN), 1)
    for q in range(SLICES):
        both = where_ref[mine, q : q + 1] & lane
        both = both ^ (both >> 4)
        both = both ^ (both >> 2)
        both = both ^ (both >> 1)
        signs = (1 - 2 * (both & 1)).astype(F32).astype(BF16)
        vals = mixed_ref[q]
        high = vals.astype(BF16)
        rest = vals - high.astype(F32)
        mid = rest.astype(BF16)
        low = (rest - mid.astype(F32)).astype(BF16)
        out = jnp.dot(signs, low, preferred_element_type=F32)
        out += jnp.dot(signs, mid, preferred_element_type=F32)
        out += jnp.dot(signs, high, preferred_element_type=F32)
        o_ref[q * 64 : (q + 1) * 64, :] = out


def sample(slices, scale):
    cols = 2 * slices.shape[2]
    half = lax.axis_index("core").reshape(1)
    return pl.pallas_call(
        lambda *refs: sample_kernel(scale, *refs),
        out_shape=jax.ShapeDtypeStruct((SLICES * 64, cols), F32),
        in_specs=[pl.BlockSpec(memory_space=pltpu.SMEM), pl.BlockSpec(memory_space=pltpu.VMEM)],
        out_specs=pl.BlockSpec(memory_space=pltpu.VMEM),
        scratch_shapes=[pltpu.VMEM((SLICES, SPAN, cols), F32), pltpu.VMEM((SPAN, SLICES), jnp.int32)],
        compiler_params=pltpu.CompilerParams(vmem_limit_bytes=12 << 20),
        name="sample",
    )(half, slices)


def early_pairs(core):
    return [((1, 0), (0, 0)), ((1, 0), (0, 1)), ((1, 0), (-1, 0)), ((0, 0), (0, core))]


def late_pairs(z):
    if z < 4:
        return [((2, 0), (0, 1)), ((1, 0), (-2, 0)), ((2, 0), (-1, 1)), ((2, 0), (-2, 0))]
    return [((2, 1), (0, 0)), ((1, 0), (-2, 0)), ((2, 1), (-1, 0)), ((2, 1), (-2, 0))]


def home(late, xh, y, core, z, xl):
    unit = (xh * 4 + y) // 2
    (rz, rx), (cz, cx) = late_pairs(z)[unit] if late else early_pairs(core)[unit]
    mirror = core == 1 and (late or unit < 3)
    row, col = ((z + rz) % 8, xl ^ rx), ((z + cz) % 8, xl ^ cx)
    if mirror:
        row, col = col, row
    return (row[0] // 4, row[0] % 4, row[1], col[0], col[1]), mirror


def arrivals():
    table = np.zeros(SIZES, np.int32)
    for here in itertools.product(*[range(s) for s in SIZES]):
        for late in (False, True):
            there, mirror = home(late, *here)
            table[there] = 2 * late + mirror
    return table.reshape(-1)


def halves(ref):
    vals = ref[...]
    high = vals.astype(BF16)
    return high, (vals - high.astype(F32)).astype(BF16)


def turned(parts):
    return tuple(v.T for v in parts)


def block(a, b):
    out = jnp.dot(a[0], b[1], preferred_element_type=F32)
    out += jnp.dot(a[1], b[0], preferred_element_type=F32)
    return out + jnp.dot(a[0], b[0], preferred_element_type=F32)


def split_block(core, out, out_ref, unit, keep_ref, send_ref, places):
    out_ref[unit] = out
    for half in range(2):
        for ref, owner in ((keep_ref, core), (send_ref, 1 - core)):
            rows = pl.ds(pl.multiple_of(half * 128 + owner * 64, 64), 64)
            ref[places[half]] = out_ref[unit, rows, :]


def early_kernel(core_ref, own_ref, beside_ref, up_ref, down_ref, keep_ref, send_ref, out_ref):
    core = core_ref[0]

    def places(unit):
        chips = (2 * unit, 2 * unit + 1)
        return [(chip % 4, slice(0, 64) if chip < 4 else slice(64, 128)) for chip in chips]

    own, beside, down = halves(own_ref), halves(beside_ref), halves(down_ref)
    up, turn = turned(halves(up_ref)), turned(own)
    for unit, right in enumerate((own, beside, down)):
        split_block(core, block(up, right), out_ref, unit, keep_ref, send_ref, places(unit))
    out_ref[3] = block(turn, own)
    out_ref[4] = block(turn, beside)
    for half in range(2):
        rows = slice(half * 128, half * 128 + 128)
        keep_ref[2 + half, 64:, :] = out_ref[3 + core, rows, :]
        send_ref[2 + half, 64:, :] = out_ref[4 - core, rows, :]
        for ref in (keep_ref, send_ref):
            ref[half, 128:, :] = jnp.zeros((64, 256), F32)


def late_kernel(
    flags_ref, own_ref, beside_ref, up_ref, down_ref, down_beside_ref, up2_ref, down2_ref, keep_ref, send_ref, out_ref, high_ref, low_ref
):
    core, low = flags_ref[0], flags_ref[1]

    def pick(k, a_ref, b_ref):
        @pl.when(low == 1)
        def _():
            high_ref[k], low_ref[k] = halves(a_ref)

        @pl.when(low == 0)
        def _():
            high_ref[k], low_ref[k] = halves(b_ref)

    pick(0, beside_ref, own_ref)
    pick(1, down_beside_ref, down_ref)
    up2, down2 = turned(halves(up2_ref)), halves(down2_ref)
    blocks = [
        (up2, (high_ref[0], low_ref[0])),
        (turned(halves(up_ref)), down2),
        (up2, (high_ref[1], low_ref[1])),
        (up2, down2),
    ]
    for unit, pair in enumerate(blocks):
        split_block(core, block(*pair), out_ref, unit, keep_ref, send_ref, (2 * unit, 2 * unit + 1))


def call_blocks(kernel, shape, flags, operands, space, scratch, cost, name):
    vmem = pl.BlockSpec(memory_space=pltpu.VMEM)
    return pl.pallas_call(
        kernel,
        out_shape=[jax.ShapeDtypeStruct((*shape, 256), F32)] * 2,
        in_specs=[pl.BlockSpec(memory_space=pltpu.SMEM)] + [pl.BlockSpec(memory_space=space)] * len(operands),
        out_specs=[vmem] * 2,
        scratch_shapes=scratch,
        compiler_params=pltpu.CompilerParams(vmem_limit_bytes=20 << 20),
        cost_estimate=pl.CostEstimate(flops=cost, bytes_accessed=cost // 400, transcendentals=0),
        name=name,
    )(flags, *operands)


def other_core(v):
    return permute(v, lambda xh, y, c, z, x: (xh, y, c + 1, z, x))


def shards(matrix, signs, picked):
    core = lax.axis_index("core")
    z = lax.axis_index("z")
    chip = lax.axis_index("xh") * 4 + lax.axis_index("y")
    samples = picked.shape[0] * 16
    slices = mix_slices(matrix, signs, picked)
    slices = lax.all_to_all(slices, EXCHANGE, 0, 0, tiled=True)
    own = sample(slices, 1.0 / samples**0.5)

    up = permute(own, lambda xh, y, c, z, x: (xh, y, c, z - 1, x))
    down = permute(own, lambda xh, y, c, z, x: (xh, y, c, z + 1, x))
    beside = permute(own, lambda xh, y, c, z, x: (xh, y, c, z, x + 1))
    up2 = permute(up, lambda xh, y, c, z, x: (xh, y, c, z - 1, x if (z - 1) % 8 < 4 else x + 1))
    down2 = permute(down, lambda xh, y, c, z, x: (xh, y, c, z + 1, x))
    down_beside = permute(down, lambda xh, y, c, z, x: (xh, y, c, z, x + 1) if z < 4 else None)

    core_flag = core.reshape(1)
    keep, send = call_blocks(early_kernel, (4, 192), core_flag, (own, beside, up, down), pltpu.VMEM, [pltpu.VMEM((5, 256, 256), F32)], 1000, "early_blocks")
    early = keep + jnp.concatenate([other_core(send[i : i + 1]) for i in range(4)])
    row = lax.axis_index("y")
    total = lax.dynamic_index_in_dim(early, row, 0, keepdims=False)
    for step in range(1, 4):
        part = lax.dynamic_index_in_dim(early, (row + step) % 4, 0, keepdims=False)
        total += permute(part, lambda xh, y, c, z, x: (xh, y + step, c, z, x))

    def by_core(mine):
        got = other_core(mine)
        return jnp.concatenate([jnp.where(core == 0, mine, got), jnp.where(core == 0, got, mine)])

    flags = jnp.stack([core, (z < 4).astype(jnp.int32)])
    keep, send = call_blocks(
        late_kernel,
        (8, 64),
        flags,
        (own, beside, up, down, down_beside, up2, down2),
        pltpu.VMEM,
        [pltpu.VMEM((4, 256, 256), F32)] + [pltpu.VMEM((2, *own.shape), BF16)] * 2,
        40_000_000_000,
        "late_blocks",
    )
    slots = lax.all_to_all(keep + other_core(send), CHIPS, 0, 0, tiled=True)
    plane = lax.axis_index("xh")
    early = jnp.where(plane == 0, total[:128], total[64:]) + permute(
        jnp.where(plane == 0, total[64:], total[:128]), lambda xh, y, c, z, x: (xh + 1, y, c, z, x)
    )
    got, rest = [], early[:64]
    for part in range(2):
        got.append(other_core(rest[part * 32 : part * 32 + 32]))
        got[-1], rest = lax.optimization_barrier((got[-1], rest))
    got, rest = jnp.concatenate(got), early[:64]
    both = jnp.concatenate([jnp.where(core == 0, rest, got), jnp.where(core == 0, got, rest)])
    early = jnp.where(chip >= 6, early, both)
    late = by_core(jnp.sum(slots, axis=0))
    even = chip % 2 == 0
    first = permute(jnp.where(even, early, late), lambda *here: home(here[1] % 2 == 1, *here)[0])
    second = permute(jnp.where(even, late, early), lambda *here: home(here[1] % 2 == 0, *here)[0])
    kind = jnp.asarray(arrivals())[lax.axis_index(NAMES)]
    swap = kind >= 2
    whole = jnp.concatenate([jnp.where(swap, second, first), jnp.where(swap, first, second)])
    return jnp.where(kind % 2 == 1, whole.T, whole)


def solution(mesh):
    mesh = Mesh(mesh.devices.reshape(SIZES), NAMES)
    return jax.shard_map(
        shards, mesh=mesh, in_specs=(P(ROW, COL), P(ROW), P(ROW)), out_specs=P(ROW, COL), check_vma=False
    )
```

```python
import itertools

import jax
import jax.numpy as jnp
import numpy as np
from jax import lax
from jax.experimental import pallas as pl
from jax.experimental.pallas import tpu as pltpu
from jax.sharding import Mesh
from jax.sharding import PartitionSpec as P

NAMES = ("xh", "y", "core", "z", "xl")
SIZES = (2, 4, 2, 8, 2)
ROW = ("xh", "y", "core")
COL = ("z", "xl")
EXCHANGE = ("y", "core", "xh")
CHIPS = ("xh", "y")
SLICES = 16
SPAN = 128
PLACE = [(s // 2 % 4 * 2 + s % 2) * 2 + s // 8 for s in range(16)]
F32 = jnp.float32
BF16 = jnp.bfloat16


def permute(block, route):
    pairs = []
    for here in itertools.product(*[range(s) for s in SIZES]):
        there = route(*here)
        if there is None:
            continue
        there = tuple(v % s for v, s in zip(there, SIZES))
        pairs.append((int(np.ravel_multi_index(here, SIZES)), int(np.ravel_multi_index(there, SIZES))))
    return lax.ppermute(block, NAMES, pairs)


def hadamard(vals):
    step = 1
    vals = list(vals)
    while step < len(vals):
        for i in range(len(vals)):
            if not i & step:
                a, b = vals[i], vals[i | step]
                vals[i], vals[i | step] = a + b, a - b
        step *= 2
    return vals


def mix_kernel(signs_ref, picked_ref, x_ref, o_ref, sign_ref, x_buf, o_buf, in_sem, out_sem):
    steps, rows = 4, SPAN // 4

    def part(ref, k):
        return ref.at[:, pl.ds(k * rows, rows), :]

    loads = [pltpu.make_async_copy(part(x_ref, k), part(x_buf, k), in_sem.at[k]) for k in range(steps)]
    for load in loads:
        load.start()
    sign_ref[...] = signs_ref[...].astype(F32).T
    for s in range(SLICES):
        row = picked_ref[s // 2 : s // 2 + 1, :].astype(F32)
        o_buf[PLACE[s], 2 * SPAN :, :] = jnp.broadcast_to(row, (8, 128))
    picks = pl.ds(2 * SPAN, 8)
    stores = [pltpu.make_async_copy(o_buf.at[:, picks, :], o_ref.at[:, picks, :], out_sem.at[0, steps])]
    stores[0].start()
    for k in range(steps):
        loads[k].wait()

        def chunk(i, carry):
            at = pl.ds(pl.multiple_of(k * rows + i * 8, 8), 8)
            sign = sign_ref[at, :]
            sign = [jnp.broadcast_to(sign[:, a : a + 1], (8, 128)) for a in range(SLICES)]
            for half in range(2):
                vals = hadamard([x_buf[a, at, half * 128 : half * 128 + 128] * sign[a] for a in range(SLICES)])
                to = pl.ds(pl.multiple_of(half * SPAN + k * rows + i * 8, 8), 8)
                for s in range(SLICES):
                    o_buf[PLACE[s], to, :] = vals[s]
            return carry

        lax.fori_loop(0, rows // 8, chunk, 0, unroll=True)
        for half in range(2):
            done = pl.ds(half * SPAN + k * rows, rows)
            stores.append(pltpu.make_async_copy(o_buf.at[:, done, :], o_ref.at[:, done, :], out_sem.at[half, k]))
            stores[-1].start()
    for store in stores:
        store.wait()


def mix_slices(matrix, signs, picked):
    rows, cols = matrix.shape
    vmem = pl.BlockSpec(memory_space=pltpu.VMEM)
    shape = (SLICES, 2 * SPAN + 8, 128)
    return pl.pallas_call(
        mix_kernel,
        out_shape=pltpu.HBM(shape, F32),
        in_specs=[vmem, vmem, pl.BlockSpec(memory_space=pltpu.HBM)],
        out_specs=pl.BlockSpec(memory_space=pltpu.HBM),
        scratch_shapes=[
            pltpu.VMEM((SPAN, SLICES), F32),
            pltpu.VMEM((SLICES, SPAN, cols), F32),
            pltpu.VMEM(shape, F32),
            pltpu.SemaphoreType.DMA((4,)),
            pltpu.SemaphoreType.DMA((2, 5)),
        ],
        name="mix_slices",
    )(
        signs.reshape(SLICES, SPAN),
        picked.reshape(8, 128),
        pltpu.with_memory_space_constraint(matrix.reshape(SLICES, SPAN, cols), pltpu.HBM),
    )


def sample_kernel(scale, half_ref, y_ref, o_ref, mixed_ref, where_ref):
    picks = jnp.concatenate([y_ref[PLACE[q], 2 * SPAN : 2 * SPAN + 1, :] for q in range(SLICES)], axis=0)
    where_ref[...] = picks.T.astype(jnp.int32)

    def chunk(i, carry):
        rows = pl.ds(pl.multiple_of(i * 8, 8), 8)
        for half in range(2):
            at = pl.ds(pl.multiple_of(half * SPAN + i * 8, 8), 8)
            vals = hadamard([y_ref[PLACE[p], at, :] for p in range(SLICES)])
            for q in range(SLICES):
                mixed_ref[q, rows, half * 128 : half * 128 + 128] = vals[q] * scale
        return carry

    lax.fori_loop(0, SPAN // 8, chunk, 0)
    mine = pl.ds(pl.multiple_of(half_ref[0] * 64, 64), 64)
    lane = lax.broadcasted_iota(jnp.int32, (64, SPAN), 1)
    for q in range(SLICES):
        both = where_ref[mine, q : q + 1] & lane
        both = both ^ (both >> 4)
        both = both ^ (both >> 2)
        both = both ^ (both >> 1)
        signs = (1 - 2 * (both & 1)).astype(F32).astype(BF16)
        vals = mixed_ref[q]
        high = vals.astype(BF16)
        rest = vals - high.astype(F32)
        mid = rest.astype(BF16)
        low = (rest - mid.astype(F32)).astype(BF16)
        out = jnp.dot(signs, low, preferred_element_type=F32)
        out += jnp.dot(signs, mid, preferred_element_type=F32)
        out += jnp.dot(signs, high, preferred_element_type=F32)
        o_ref[q * 64 : (q + 1) * 64, :] = out


def sample(slices, scale):
    cols = 2 * slices.shape[2]
    half = lax.axis_index("core").reshape(1)
    return pl.pallas_call(
        lambda *refs: sample_kernel(scale, *refs),
        out_shape=jax.ShapeDtypeStruct((SLICES * 64, cols), F32),
        in_specs=[pl.BlockSpec(memory_space=pltpu.SMEM), pl.BlockSpec(memory_space=pltpu.VMEM)],
        out_specs=pl.BlockSpec(memory_space=pltpu.VMEM),
        scratch_shapes=[pltpu.VMEM((SLICES, SPAN, cols), F32), pltpu.VMEM((SPAN, SLICES), jnp.int32)],
        compiler_params=pltpu.CompilerParams(vmem_limit_bytes=12 << 20),
        name="sample",
    )(half, slices)


def early_pairs(core):
    return [((1, 0), (0, 0)), ((1, 0), (0, 1)), ((1, 0), (-1, 0)), ((0, 0), (0, core))]


def late_pairs(z):
    if z < 4:
        return [((2, 0), (0, 1)), ((1, 0), (-2, 0)), ((2, 0), (-1, 1)), ((2, 0), (-2, 0))]
    return [((2, 1), (0, 0)), ((1, 0), (-2, 0)), ((2, 1), (-1, 0)), ((2, 1), (-2, 0))]


def home(late, xh, y, core, z, xl):
    unit = (xh * 4 + y) // 2
    (rz, rx), (cz, cx) = late_pairs(z)[unit] if late else early_pairs(core)[unit]
    mirror = core == 1 and (late or unit < 3)
    row, col = ((z + rz) % 8, xl ^ rx), ((z + cz) % 8, xl ^ cx)
    if mirror:
        row, col = col, row
    return (row[0] // 4, row[0] % 4, row[1], col[0], col[1]), mirror


def arrivals():
    table = np.zeros(SIZES, np.int32)
    for here in itertools.product(*[range(s) for s in SIZES]):
        for late in (False, True):
            there, mirror = home(late, *here)
            table[there] = 2 * late + mirror
    return table.reshape(-1)


def halves(ref):
    vals = ref[...]
    high = vals.astype(BF16)
    return high, (vals - high.astype(F32)).astype(BF16)


def turned(parts):
    return tuple(v.T for v in parts)


def block(a, b):
    out = jnp.dot(a[0], b[1], preferred_element_type=F32)
    out += jnp.dot(a[1], b[0], preferred_element_type=F32)
    return out + jnp.dot(a[0], b[0], preferred_element_type=F32)


def split_block(core, out, out_ref, unit, keep_ref, send_ref, places):
    out_ref[unit] = out
    for half in range(2):
        for ref, owner in ((keep_ref, core), (send_ref, 1 - core)):
            rows = pl.ds(pl.multiple_of(half * 128 + owner * 64, 64), 64)
            ref[places[half]] = out_ref[unit, rows, :]


def early_kernel(core_ref, own_ref, beside_ref, up_ref, down_ref, keep_ref, send_ref, out_ref):
    core = core_ref[0]

    def places(unit):
        chips = (2 * unit, 2 * unit + 1)
        return [(chip % 4, slice(0, 64) if chip < 4 else slice(64, 128)) for chip in chips]

    own, beside, down = halves(own_ref), halves(beside_ref), halves(down_ref)
    up, turn = turned(halves(up_ref)), turned(own)
    for unit, right in enumerate((own, beside, down)):
        split_block(core, block(up, right), out_ref, unit, keep_ref, send_ref, places(unit))
    out_ref[3] = block(turn, own)
    out_ref[4] = block(turn, beside)
    for half in range(2):
        rows = slice(half * 128, half * 128 + 128)
        keep_ref[2 + half, 64:, :] = out_ref[3 + core, rows, :]
        send_ref[2 + half, 64:, :] = out_ref[4 - core, rows, :]
        for ref in (keep_ref, send_ref):
            ref[half, 128:, :] = jnp.zeros((64, 256), F32)


def late_kernel(
    flags_ref, own_ref, beside_ref, up_ref, down_ref, down_beside_ref, up2_ref, down2_ref, keep_ref, send_ref, out_ref, high_ref, low_ref
):
    core, low = flags_ref[0], flags_ref[1]

    def pick(k, a_ref, b_ref):
        @pl.when(low == 1)
        def _():
            high_ref[k], low_ref[k] = halves(a_ref)

        @pl.when(low == 0)
        def _():
            high_ref[k], low_ref[k] = halves(b_ref)

    pick(0, beside_ref, own_ref)
    pick(1, down_beside_ref, down_ref)
    up2, down2 = turned(halves(up2_ref)), halves(down2_ref)
    blocks = [
        (up2, (high_ref[0], low_ref[0])),
        (turned(halves(up_ref)), down2),
        (up2, (high_ref[1], low_ref[1])),
        (up2, down2),
    ]
    for unit, pair in enumerate(blocks):
        split_block(core, block(*pair), out_ref, unit, keep_ref, send_ref, (2 * unit, 2 * unit + 1))


def call_blocks(kernel, shape, flags, operands, space, scratch, cost, name):
    vmem = pl.BlockSpec(memory_space=pltpu.VMEM)
    return pl.pallas_call(
        kernel,
        out_shape=[jax.ShapeDtypeStruct((*shape, 256), F32)] * 2,
        in_specs=[pl.BlockSpec(memory_space=pltpu.SMEM)] + [pl.BlockSpec(memory_space=space)] * len(operands),
        out_specs=[vmem] * 2,
        scratch_shapes=scratch,
        compiler_params=pltpu.CompilerParams(vmem_limit_bytes=14 << 20),
        cost_estimate=pl.CostEstimate(flops=cost, bytes_accessed=cost // 400, transcendentals=0),
        name=name,
    )(flags, *operands)


def other_core(v):
    return permute(v, lambda xh, y, c, z, x: (xh, y, c + 1, z, x))


def shards(matrix, signs, picked):
    core = lax.axis_index("core")
    z = lax.axis_index("z")
    chip = lax.axis_index("xh") * 4 + lax.axis_index("y")
    samples = picked.shape[0] * 16
    slices = mix_slices(matrix, signs, picked)
    slices = lax.all_to_all(slices, EXCHANGE, 0, 0, tiled=True)
    own = sample(slices, 1.0 / samples**0.5)

    up = permute(own, lambda xh, y, c, z, x: (xh, y, c, z - 1, x))
    down = permute(own, lambda xh, y, c, z, x: (xh, y, c, z + 1, x))
    beside = permute(own, lambda xh, y, c, z, x: (xh, y, c, z, x + 1))
    up2 = permute(up, lambda xh, y, c, z, x: (xh, y, c, z - 1, x if (z - 1) % 8 < 4 else x + 1))
    down2 = permute(down, lambda xh, y, c, z, x: (xh, y, c, z + 1, x))
    down_beside = permute(down, lambda xh, y, c, z, x: (xh, y, c, z, x + 1) if z < 4 else None)

    core_flag = core.reshape(1)
    keep, send = call_blocks(early_kernel, (4, 192), core_flag, (own, beside, up, down), pltpu.VMEM, [pltpu.VMEM((5, 256, 256), F32)], 1000, "early_blocks")
    early = keep + jnp.concatenate([other_core(send[i : i + 1]) for i in range(4)])
    row = lax.axis_index("y")
    total = lax.dynamic_index_in_dim(early, row, 0, keepdims=False)
    for step in range(1, 4):
        part = lax.dynamic_index_in_dim(early, (row + step) % 4, 0, keepdims=False)
        total += permute(part, lambda xh, y, c, z, x: (xh, y + step, c, z, x))

    def by_core(mine):
        got = other_core(mine)
        return jnp.concatenate([jnp.where(core == 0, mine, got), jnp.where(core == 0, got, mine)])

    flags = jnp.stack([core, (z < 4).astype(jnp.int32)])
    keep, send = call_blocks(
        late_kernel,
        (8, 64),
        flags,
        (own, beside, up, down, down_beside, up2, down2),
        pltpu.VMEM,
        [pltpu.VMEM((4, 256, 256), F32)] + [pltpu.VMEM((2, *own.shape), BF16)] * 2,
        40_000_000_000,
        "late_blocks",
    )
    slots = lax.all_to_all(keep + other_core(send), CHIPS, 0, 0, tiled=True)
    plane = lax.axis_index("xh")
    early = jnp.where(plane == 0, total[:128], total[64:]) + permute(
        jnp.where(plane == 0, total[64:], total[:128]), lambda xh, y, c, z, x: (xh + 1, y, c, z, x)
    )
    got, rest = [], early[:64]
    for part in range(2):
        got.append(other_core(rest[part * 32 : part * 32 + 32]))
        got[-1], rest = lax.optimization_barrier((got[-1], rest))
    got, rest = jnp.concatenate(got), early[:64]
    both = jnp.concatenate([jnp.where(core == 0, rest, got), jnp.where(core == 0, got, rest)])
    early = jnp.where(chip >= 6, early, both)
    late = by_core(jnp.sum(slots, axis=0))
    even = chip % 2 == 0
    first = permute(jnp.where(even, early, late), lambda *here: home(here[1] % 2 == 1, *here)[0])
    second = permute(jnp.where(even, late, early), lambda *here: home(here[1] % 2 == 0, *here)[0])
    kind = jnp.asarray(arrivals())[lax.axis_index(NAMES)]
    swap = kind >= 2
    whole = jnp.concatenate([jnp.where(swap, second, first), jnp.where(swap, first, second)])
    return jnp.where(kind % 2 == 1, whole.T, whole)


def solution(mesh):
    mesh = Mesh(mesh.devices.reshape(SIZES), NAMES)
    return jax.shard_map(
        shards, mesh=mesh, in_specs=(P(ROW, COL), P(ROW), P(ROW)), out_specs=P(ROW, COL), check_vma=False
    )
```
